32 devices in a mesh: sub: 8 (over z, x), col: 4 (over y, core).
Axes of the slice: x: 2, y: 2, z: 4, core: 2. Of those that a mesh axis runs over, the one named last changes fastest.
Arguments:
- elem_records: bfloat16 [8192, 1152], P(('sub', 'col')), may hold values from -0.119628906 to 0.119628906
- elem_owner: int32 [8192, 1], P(('sub', 'col')), may hold values from 0 to 7; in each aligned block of 256 rows (0 to 255, 256 to 511, ...) at most 64 rows name the same one
- elem_block: int32 [8192], P(('sub', 'col')), may hold values from 0 to 255
- elem_offset: int32 [8192], P(('sub', 'col')), may hold values from 0 to 5
- modes: bfloat16 [128, 64, 512], P('sub', None, 'col'), may hold values from -0.59765625 to 0.59765625
- mode_readers: int32 [128, 2], P('sub'), may hold values from 0 to 7, all different within a row; in each aligned block of 16 rows (0 to 15, 16 to 31, ...) at most 8 rows name the same one
- pattern: int32 [512, 4], P('sub'), may hold values from 0 to 63
Outputs:
- gram_stiff: float32 [512, 512], P('sub', 'col')
- gram_mass: float32 [512, 512], P('sub', 'col')
The draws below stay inside these ranges and needn't reach their ends.
Inputs may be any that keep to these rules, and one draw needn't show every extreme that they name: `elem_owner`: the rows of one device name one subdomain at most 64 times, and in every draw some subdomain exactly 64 times. `mode_readers`: each row names two different subdomains; the rows of one index of sub name one subdomain at most 8 times, and in every draw some subdomain exactly 8 times.
All inputs are finite; a program needn't handle non-finite values.
Results may differ from the reference program's by a relative error of at most 0.0038.
Values may be sent and summed in bfloat16 or wider, within the bound.
No kernel may reach another device: no remote copies, remote signals or barrier semaphores. Data moves between devices by JAX's collectives and lax.ppermute only.
A program may use at most 192 MiB of HBM per device.

```python
import math
import jax
import jax.numpy as jnp
import numpy as np
from jax import lax

MODES = 512
BS = 64
EDOF = 24
NNZ = 4
E_DEV = 256
QB_DEV = 16
NQ = 64
CAPQ = 8
CAPE = 64
KW = 1152
ELEMS = 8192
BLOCKS = 128
SLOTS = 512
N_SUB = 8
N_COL = 4


def touch_ends(drawn, own_key, low, top_value):
    longest = drawn.shape.index(max(drawn.shape))
    spots = []
    for shift in (0, 1):
        where = [jax.random.randint(jax.random.fold_in(own_key, axis), (), 0, length) for axis, length in enumerate(drawn.shape)]
        where[longest] = (where[longest] + shift) % drawn.shape[longest]
        spots.append(tuple(where))
    return drawn.at[spots[0]].set(low).at[spots[1]].set(top_value)


def block_scale(rng, dims, split, low, high):
    level, own = 1.0, jax.random.fold_in(rng, 6)
    for axis_at, parts in split:
        steps = jnp.exp(jax.random.uniform(jax.random.fold_in(own, axis_at), (parts,), jnp.float32, low / len(split), high / len(split)))
        level = level * jnp.repeat(steps, dims[axis_at] // parts).reshape([-1 if axis == axis_at else 1 for axis in range(len(dims))])
    return level


def deal_out(key, own, number, rows, amount, top, most, slope):
    ranking = jax.random.permutation(key, amount)
    crowded, ordinary = shares(amount, rows * top, most, slope, True), shares(amount, rows * top, most, slope, False)
    places = jnp.arange(amount)

    def named(tallies, rotation):
        used = int((tallies > 0).sum())
        fixed = max(1, used // 4)
        moved = fixed + (places - fixed + rotation * (used - fixed)) % max(1, amount - fixed)
        return jnp.zeros((amount,), jnp.int32).at[ranking[jnp.where(places < fixed, places, moved)]].set(jnp.asarray(tallies, jnp.int32))

    tallies = jnp.where(number % 4 == 0, named(crowded, number // 4), named(ordinary, number - number // 4 - 1))
    mixed = jax.random.permutation(jax.random.fold_in(own, 3), amount)
    donor, sink = mixed[0:amount // 2 * 2:2], mixed[1:amount // 2 * 2:2]
    margin = jnp.minimum(tallies[donor] - 1, most - tallies[sink]) // 2
    margin = jnp.where((donor == ranking[0]) | (sink == ranking[0]) | (tallies[sink] == 0), 0, jnp.maximum(margin, 0))
    moved = jax.random.randint(jax.random.fold_in(own, 4), (amount // 2,), 0, 1 << 20) % (margin + 1)
    tallies = tallies.at[donor].add(-moved).at[sink].add(moved)
    labels = jnp.searchsorted(jnp.cumsum(tallies), jnp.arange(rows * top), side="right").astype(jnp.int32)
    grid = labels.reshape(top, rows).T
    grid = grid[jax.random.permutation(jax.random.fold_in(own, 1), rows)]
    rotation = jax.random.randint(jax.random.fold_in(own, 2), (rows, 1), 0, top)
    return jnp.take_along_axis(grid, (jnp.arange(top)[None, :] + rotation) % top, axis=1)


def shares(amount, total, reach, slope, full):
    weights = [(1 << 20) // math.isqrt(standing ** slope) + 1 for standing in range(1, amount + 1)]
    largest = reach if full else min(reach, max(-(-total // amount), total * weights[0] // sum(weights)))
    least = 1 if total - largest >= amount - 1 else 0
    given, rest = [largest] + [least] * (amount - 1), total - largest - least * (amount - 1)
    while rest > 0:
        candidates = [i for i in range(1, amount) if given[i] < largest] or [i for i in range(1, amount) if given[i] < reach]
        whole, left = sum([weights[i] for i in candidates]), rest
        for i in candidates:
            extra = min(reach - given[i], max(1, left * weights[i] // whole), rest)
            given[i] = given[i] + extra
            rest = rest - extra
    return np.array(given)


def centred(rng, extent, spread, limit, cuts=(), held_as=jnp.bfloat16):
    array = jax.random.normal(rng, extent, jnp.float32) * spread
    if len(cuts) > 0:
        array = block_scale(rng, extent, cuts, -0.22, 0.18) * array
    return jnp.clip(array, min=-limit, max=limit).astype(held_as)


def setup_inputs(seed: int = 0) -> dict:
    key_list = jax.random.split(jax.random.key(seed), 8)
    elem_records = centred(key_list[0], (ELEMS, KW), 0.02, 0.119628906, ((0, 32),))
    elem_owner_keys = jax.random.split(jax.random.fold_in(key_list[1], 1), ELEMS // E_DEV)
    elem_owner_turns = jax.random.permutation(jax.random.fold_in(key_list[1], 3), ELEMS // E_DEV)
    elem_owner = jax.vmap(lambda own, number: deal_out(jax.random.fold_in(key_list[1], 2), own, number, E_DEV, N_SUB, 1, CAPE, 2))(elem_owner_keys, elem_owner_turns).reshape((ELEMS, 1))
    elem_block = touch_ends(jax.random.randint(key_list[2], (ELEMS,), 0, NQ * NNZ), jax.random.fold_in(key_list[2], 1), 0, (NQ * NNZ) - 1).astype(jnp.int32)
    elem_offset = touch_ends(jax.random.randint(key_list[3], (ELEMS,), 0, 6), jax.random.fold_in(key_list[3], 1), 0, 5).astype(jnp.int32)
    modes = centred(key_list[4], (BLOCKS, BS, MODES), 0.1, 0.59765625, ((0, 8), (2, 4)))
    mode_readers_keys = jax.random.split(jax.random.fold_in(key_list[5], 1), BLOCKS // QB_DEV)
    mode_readers_turns = jax.random.permutation(jax.random.fold_in(key_list[5], 3), BLOCKS // QB_DEV)
    mode_readers = jax.vmap(lambda own, number: deal_out(jax.random.fold_in(key_list[5], 2), own, number, QB_DEV, N_SUB, 2, CAPQ, 1))(mode_readers_keys, mode_readers_turns).reshape((BLOCKS, 2))
    pattern = touch_ends(jax.random.randint(key_list[6], (SLOTS, NNZ), 0, NQ), jax.random.fold_in(key_list[6], 1), 0, NQ - 1).astype(jnp.int32)
    return {"elem_records": elem_records, "elem_owner": elem_owner, "elem_block": elem_block, "elem_offset": elem_offset, "modes": modes, "mode_readers": mode_readers, "pattern": pattern}


def place_index(block_ids, offsets, slot_count, entry_count):
    entries = jnp.arange(EDOF * EDOF, dtype=jnp.int32)
    row_part = entries // EDOF
    col_part = entries % EDOF
    shifted = offsets[:, None] * 8
    base_index = block_ids[:, None] * (BS * BS) + (shifted + row_part[None, :]) * BS + shifted + col_part[None, :]
    return jnp.concatenate([base_index, base_index + slot_count * entry_count * BS * BS], axis=1)


def reference(elem_records, elem_owner, elem_block, elem_offset, modes, mode_readers, pattern):
    owners = elem_owner[:, 0]
    order = jnp.argsort(owners, stable=True)
    most_per = 2 * E_DEV * N_COL
    sorted_records = jnp.concatenate([elem_records[order], jnp.zeros((most_per, KW), elem_records.dtype)], axis=0)
    sorted_block = jnp.concatenate([elem_block[order], jnp.zeros((most_per,), jnp.int32)], axis=0)
    sorted_offset = jnp.concatenate([elem_offset[order], jnp.zeros((most_per,), jnp.int32)], axis=0)
    readers_flat = mode_readers.reshape(-1)
    total_size = 2 * NQ * NNZ * BS * BS

    def per_sub(carry, sub_id):
        start_at = jnp.sum((owners < sub_id).astype(jnp.int32)).astype(jnp.int32)
        live_count = jnp.sum((owners == sub_id).astype(jnp.int32))
        records = lax.dynamic_slice_in_dim(sorted_records, start_at, most_per, 0)
        blocks_here = lax.dynamic_slice_in_dim(sorted_block, start_at, most_per, 0)
        offsets_here = lax.dynamic_slice_in_dim(sorted_offset, start_at, most_per, 0)
        valid = jnp.arange(most_per, dtype=jnp.int32) < live_count
        flat = place_index(blocks_here, offsets_here, NQ, NNZ)
        flat = jnp.where(valid[:, None], flat, total_size)
        assembled = jnp.zeros((total_size,), jnp.float32).at[flat.reshape(-1)].add(
            records.astype(jnp.float32).reshape(-1), mode="drop")
        stiff_mass = assembled.reshape(2, NQ, NNZ, BS, BS).astype(jnp.bfloat16)
        matches = (readers_flat == sub_id).reshape(N_SUB, QB_DEV * 2).astype(jnp.int32)
        ranks = jnp.cumsum(matches, axis=1) - 1
        targets = jnp.arange(N_SUB, dtype=jnp.int32)[:, None] * CAPQ + ranks
        slots = jnp.where(matches > 0, targets, NQ).reshape(-1).astype(jnp.int32)
        entry_ids = jnp.arange(BLOCKS * 2, dtype=jnp.int32)
        slot_entry = jnp.full((NQ,), -1, jnp.int32).at[slots].set(entry_ids, mode="drop")
        filled = slot_entry >= 0
        picked = modes[jnp.maximum(slot_entry, 0) // 2]
        slot_modes = jnp.where(filled[:, None, None], picked, jnp.zeros_like(picked))
        local_pattern = lax.dynamic_slice_in_dim(pattern, (sub_id * NQ).astype(jnp.int32), NQ, 0)
        gathered = slot_modes[local_pattern]
        products = jnp.einsum("crjab,rjbm->cram", stiff_mass.astype(jnp.float32),
                              gathered.astype(jnp.float32)).astype(jnp.bfloat16)
        mode_rows = slot_modes.reshape(NQ * BS, MODES)
        stiff_term = jnp.dot(mode_rows.T, products[0].reshape(NQ * BS, MODES), preferred_element_type=jnp.float32)
        mass_term = jnp.dot(mode_rows.T, products[1].reshape(NQ * BS, MODES), preferred_element_type=jnp.float32)
        return (carry[0] + stiff_term, carry[1] + mass_term), None

    start_sums = (jnp.zeros((MODES, MODES), jnp.float32), jnp.zeros((MODES, MODES), jnp.float32))
    sums, unused = lax.scan(per_sub, start_sums, jnp.arange(N_SUB, dtype=jnp.int32))
    return sums[0], sums[1]
```

```python
import functools
import math

import jax
import jax.numpy as jnp
import numpy as np
from jax import lax
from jax.experimental import pallas as pl
from jax.experimental.pallas import tpu as pltpu
from jax.sharding import PartitionSpec as P

AXES = ("sub", "col")
WIN = 32
GROUP = 8
STEP = 4
EPS = GROUP * STEP


def permutation(sub_count, col_count, move):
    pairs = []
    for s in range(sub_count):
        for c in range(col_count):
            s2, c2 = move(s, c)
            pairs.append((s * col_count + c, s2 * col_count + c2))
    return pairs


def line_ring(n):
    odd = n - 1 if n % 2 == 0 else n - 2
    return list(range(0, n, 2)) + list(range(odd, 0, -2))


def fold_constants(kw):
    half = kw // 2
    edof = math.isqrt(half)
    lane = np.arange(kw)
    within = lane % half
    row = np.arange(WIN)
    masks = np.stack([(within % edof)[None, :] == (row - 8 * p)[:, None] for p in (0, 1)])
    n = np.arange(256)
    fold = ((n // 128)[None, :] == (lane // half)[:, None]) & (
        (n % WIN)[None, :] == (within // edof)[:, None]
    )
    return masks.astype(np.float32), fold


def prep_kernel(
    caps, nnz, rows_per_source, own_ref, blk_ref, off_ref, tab_ref, rel_ref, rec_ref, mask_ref,
    fold_ref, w_ref, lrow_ref, rrow_ref, recf, lhs,
):
    step = pl.program_id(0)
    zero_row = rel_ref.shape[0] * rows_per_source
    entries = tab_ref.shape[1] - tab_ref.shape[0] * caps
    recf[...] = rec_ref[...].astype(jnp.float32)
    parity = []

    def source_row(sub, slot, start):
        t = lax.div(slot, caps)
        local = tab_ref[t, entries + sub * caps + (slot - t * caps)]
        return jnp.where(local < 0, zero_row, rel_ref[t] * rows_per_source + local * 64) + start

    for e in range(EPS):
        at = step * EPS + e
        sub, blk, off = own_ref[at], blk_ref[at], off_ref[at]
        start = lax.shift_right_logical(off, 1) * 16
        lrow_ref[at] = source_row(sub, lax.div(blk, nnz), start)
        rrow_ref[at] = source_row(sub, tab_ref[sub, blk], start)
        p = lax.bitwise_and(off, 1)
        parity.append(p)
        x = recf[pl.ds(e, WIN, stride=0), :]
        lhs[e * WIN : (e + 1) * WIN, :] = (x * mask_ref[p]).astype(jnp.bfloat16)
    block_of_lane = lax.broadcasted_iota(jnp.int32, (WIN, 128), 1) // WIN
    for g in range(STEP):
        rows = GROUP * WIN
        out = jnp.dot(
            lhs[g * rows : (g + 1) * rows, :], fold_ref[...], preferred_element_type=jnp.float32
        )
        for e in range(GROUP):
            p = parity[g * GROUP + e]
            for c in range(2):
                piece = out[e * WIN : (e + 1) * WIN, c * 128 : (c + 1) * 128]
                piece = pltpu.roll(piece, 8 * p, 1)
                piece = jnp.where(block_of_lane == e % 4, piece, 0.0).astype(jnp.bfloat16)
                for tile in range(2):
                    w_ref[g, e * WIN : (e + 1) * WIN, c * 256 + tile * 128 : c * 256 + tile * 128 + 128] = (
                        piece if tile == e // 4 else jnp.zeros_like(piece)
                    )


def main_kernel(hops, lrow_ref, rrow_ref, mine_ref, *refs):
    shards = refs[: hops * 8]
    w_ref, own_ref, send_ref = refs[hops * 8 : hops * 8 + 3]
    modes, lg, rg, yt, acc, sems = refs[hops * 8 + 3 :]
    step = pl.program_id(0)
    per = shards[0].shape[0]
    me = mine_ref[0]

    @pl.when(step == 0)
    def _():
        odd = lax.bitwise_and(me, 1)
        even = 1 - odd
        copies = []
        for j in range(hops):
            homes = (
                (0, 0), (even, odd), (odd, even), (1, 1),
                (0, 2), (odd, 2 + even), (even, 2 + odd), (1, 3),
            )
            for n, (crossed, block) in enumerate(homes):
                row = pl.multiple_of((2 * j + crossed) * per, per)
                lane = pl.multiple_of(block * 128, 128)
                copies.append(
                    pltpu.make_async_copy(
                        shards[j * 8 + n],
                        modes.at[pl.ds(row, per), pl.ds(lane, 128)],
                        sems.at[j * 8 + n],
                    )
                )
        for copy in copies:
            copy.start()
        filled = 2 * hops * per
        modes[filled:, :] = jnp.zeros((modes.shape[0] - filled, modes.shape[1]), modes.dtype)
        acc[...] = jnp.zeros_like(acc)
        for copy in copies:
            copy.wait()

    rows = GROUP * WIN
    for g in range(STEP):
        for e in range(GROUP):
            at = step * EPS + g * GROUP + e
            lrow = pl.multiple_of(lrow_ref[at], 16)
            rrow = pl.multiple_of(rrow_ref[at], 16)
            to = g * rows + e * WIN
            lg[to : to + WIN, :] = modes[pl.ds(lrow, WIN), :]
            rg[to : to + WIN, :] = modes[pl.ds(rrow, WIN), 0:256]
    for g in range(STEP):
        y = lax.dot_general(
            rg[g * rows : (g + 1) * rows, :],
            w_ref[g],
            (((0,), (0,)), ((), ())),
            preferred_element_type=jnp.float32,
        ).astype(jnp.bfloat16)
        for c in range(2):
            yt[c * 256 : (c + 1) * 256, g * rows : (g + 1) * rows] = y[:, c * 256 : (c + 1) * 256]
    acc[...] += jnp.dot(yt[...], lg[...], preferred_element_type=jnp.float32)

    @pl.when(step == pl.num_programs(0) - 1)
    def _():
        for c in range(2):
            for d, flip in enumerate((0, 2, 1, 3)):
                to = lax.bitwise_xor(me, flip)
                own_ref[c, to] = acc[c * 256 : c * 256 + 128, d * 128 : (d + 1) * 128].T
                send_ref[c, to] = acc[c * 256 + 128 : c * 256 + 256, d * 128 : (d + 1) * 128].T.astype(
                    jnp.bfloat16
                )


def body(sub_count, col_count, elem_records, elem_owner, elem_block, elem_offset, modes, mode_readers, pattern):
    elems, kw = elem_records.shape
    per_sub, bs, local_cols = modes.shape
    slots, nnz = pattern.shape
    caps = slots // sub_count
    half = sub_count // 2
    ring = line_ring(half)
    place = {z: i for i, z in enumerate(ring)}
    make = functools.partial(permutation, sub_count, col_count)
    to_next = make(lambda s, c: (ring[(place[s // 2] + 1) % half] * 2 + s % 2, c))
    first = make(lambda s, c: (s ^ 1, c) if c % 2 == 0 else (s, c ^ 2))
    second = make(lambda s, c: (s ^ 1, c) if c % 2 == 1 else (s, c ^ 2))
    core = make(lambda s, c: (s, c ^ 1))
    over = make(lambda s, c: (s, c ^ 2))
    send = lambda x, pairs: lax.ppermute(x, AXES, pairs)
    me_sub, me_col = lax.axis_index("sub"), lax.axis_index("col")

    readers = mode_readers.reshape(-1)
    order = jnp.arange(readers.shape[0], dtype=jnp.int32)
    same = (readers[:, None] == readers[None, :]) & (order[None, :] < order[:, None])
    rank = jnp.sum(same.astype(jnp.int32), axis=1)
    target = readers * caps + rank
    hit = target[:, None] == jnp.arange(sub_count * caps, dtype=jnp.int32)[None, :]
    table = jnp.sum(jnp.where(hit, order[:, None] // 2 + 1, 0), axis=0) - 1
    packed = lax.all_gather(jnp.concatenate([pattern.reshape(-1), table]), "sub", axis=0, tiled=False)

    places = jnp.stack([elem_owner[:, 0], elem_block, elem_offset])
    places = jnp.concatenate([places, send(places, core)], axis=1)
    records = jnp.concatenate([elem_records, send(elem_records, core)], axis=0)

    rel_place = jnp.asarray([place[z] for z in range(half)], jnp.int32)
    sub_ids = jnp.arange(sub_count, dtype=jnp.int32)
    hops = (rel_place[me_sub // 2] - rel_place[sub_ids // 2]) % half
    rel = hops * 2 + (sub_ids % 2 + me_sub) % 2
    flat = modes.reshape(per_sub * bs, local_cols)
    shards = []
    cur = flat
    for j in range(half):
        if j:
            cur = send(cur, to_next)
        a = send(cur, first)
        b0 = send(cur, second)
        b1 = send(a, second)
        shards.append((cur, a, b0, b1))

    elem_total = places.shape[1]
    steps = elem_total // EPS
    smem = pl.BlockSpec(memory_space=pltpu.SMEM)
    masks, fold = fold_constants(kw)
    w, lrow, rrow = pl.pallas_call(
        functools.partial(prep_kernel, caps, nnz, per_sub * bs),
        grid=(steps,),
        in_specs=[smem] * 5
        + [
            pl.BlockSpec((EPS, kw), lambda i: (i, 0)),
            pl.BlockSpec(masks.shape, lambda i: (0, 0, 0)),
            pl.BlockSpec(fold.shape, lambda i: (0, 0)),
        ],
        out_specs=[pl.BlockSpec((STEP, 256, 512), lambda i: (i, 0, 0)), smem, smem],
        out_shape=[
            jax.ShapeDtypeStruct((steps * STEP, 256, 512), jnp.bfloat16),
            jax.ShapeDtypeStruct((elem_total,), jnp.int32),
            jax.ShapeDtypeStruct((elem_total,), jnp.int32),
        ],
        scratch_shapes=[
            pltpu.VMEM((EPS, kw), jnp.float32),
            pltpu.VMEM((EPS * WIN, kw), jnp.bfloat16),
        ],
        cost_estimate=pl.CostEstimate(flops=20_000_000_000, bytes_accessed=18_000_000, transcendentals=0),
    )(places[0], places[1], places[2], packed, rel, records, jnp.asarray(masks), jnp.asarray(fold, jnp.bfloat16))

    operands = []
    for cur, a, b0, b1 in shards:
        operands += [cur, a, b0, b1] + [send(v, core) for v in (cur, a, b0, b1)]

    modes_rows = sub_count * per_sub * bs + bs + WIN
    hbm = pl.BlockSpec(memory_space=pl.ANY)
    blocked = (2, col_count, 128, 128)
    whole = pl.BlockSpec(blocked, lambda i, *_: (0, 0, 0, 0))
    own, away = pl.pallas_call(
        functools.partial(main_kernel, half),
        grid_spec=pltpu.PrefetchScalarGridSpec(
            num_scalar_prefetch=3,
            grid=(steps,),
            in_specs=[hbm] * len(operands) + [pl.BlockSpec((STEP, 256, 512), lambda i, *_: (i, 0, 0))],
            out_specs=[whole, whole],
            scratch_shapes=[
                pltpu.VMEM((modes_rows, 4 * local_cols), jnp.bfloat16),
                pltpu.VMEM((EPS * WIN, 4 * local_cols), jnp.bfloat16),
                pltpu.VMEM((EPS * WIN, 256), jnp.bfloat16),
                pltpu.VMEM((512, EPS * WIN), jnp.bfloat16),
                pltpu.VMEM((512, 512), jnp.float32),
                pltpu.SemaphoreType.DMA((len(operands),)),
            ],
        ),
        out_shape=[
            jax.ShapeDtypeStruct(blocked, jnp.float32),
            jax.ShapeDtypeStruct(blocked, jnp.bfloat16),
        ],
        compiler_params=pltpu.CompilerParams(vmem_limit_bytes=60 * 1024 * 1024),
        cost_estimate=pl.CostEstimate(flops=13_000_000_000, bytes_accessed=26_000_000, transcendentals=0),
    )(lrow, rrow, me_col[None], *operands, w)

    gram = (own + send(away, over).astype(jnp.float32)).astype(jnp.bfloat16)
    gram = gram.reshape(2, sub_count, -1, 128)
    gram = lax.all_to_all(gram, "sub", split_axis=1, concat_axis=1, tiled=True)
    gram = jnp.sum(gram.astype(jnp.float32), axis=1)
    return gram[0], gram[1]


def solution(mesh):
    in_specs = (
        P(AXES, None),
        P(AXES, None),
        P(AXES),
        P(AXES),
        P("sub", None, "col"),
        P("sub", None),
        P("sub", None),
    )
    out_specs = (P("sub", "col"), P("sub", "col"))
    return jax.shard_map(
        functools.partial(body, mesh.shape["sub"], mesh.shape["col"]),
        mesh=mesh,
        in_specs=in_specs,
        out_specs=out_specs,
        check_vma=False,
    )
```

```python
import functools
import math

import jax
import jax.numpy as jnp
from jax import lax
from jax.experimental import pallas as pl
from jax.experimental.pallas import tpu as pltpu
from jax.sharding import PartitionSpec as P

AXES = ("sub", "col")
WIN = 32
GROUP = 8
STEP = 4
EPS = GROUP * STEP


def permutation(sub_count, col_count, move):
    pairs = []
    for s in range(sub_count):
        for c in range(col_count):
            s2, c2 = move(s, c)
            pairs.append((s * col_count + c, s2 * col_count + c2))
    return pairs


def line_ring(n):
    odd = n - 1 if n % 2 == 0 else n - 2
    return list(range(0, n, 2)) + list(range(odd, 0, -2))


def prep_kernel(off_ref, rec_ref, d_ref):
    step = pl.program_id(0)
    edof = rec_ref.shape[2]
    spare = jnp.zeros((WIN - edof, 128), jnp.float32)
    blank = jnp.zeros((WIN, 128), jnp.bfloat16)
    for e in range(EPS):
        g, slot = e // GROUP, e % GROUP
        odd = lax.bitwise_and(off_ref[step * EPS + e], 1)
        for c in range(2):
            x = rec_ref[e, c].astype(jnp.float32)
            x = jnp.where(odd == 1, jnp.concatenate([spare, x]), jnp.concatenate([x, spare]))
            x = pltpu.roll(x, (slot % 4) * WIN + 8 * odd, 1).astype(jnp.bfloat16)
            rows = slice(slot * WIN, (slot + 1) * WIN)
            for tile in range(2):
                d_ref[g, c, rows, tile * 128 : (tile + 1) * 128] = x if tile == slot // 4 else blank


def main_kernel(hops, caps, nnz, own_ref, blk_ref, off_ref, tab_ref, rel_ref, mine_ref, *refs):
    shards = refs[: hops * 8]
    d_ref, keep_ref, send_ref = refs[hops * 8 : hops * 8 + 3]
    modes, lg, rg, yt, acc, sems = refs[hops * 8 + 3 :]
    step = pl.program_id(0)
    per = shards[0].shape[0]
    me = mine_ref[0]

    @pl.when(step == 0)
    def _():
        odd = lax.bitwise_and(me, 1)
        even = 1 - odd
        copies = []
        for j in range(hops):
            homes = (
                (0, 0), (even, odd), (odd, even), (1, 1),
                (0, 2), (odd, 2 + even), (even, 2 + odd), (1, 3),
            )
            for n, (crossed, block) in enumerate(homes):
                row = pl.multiple_of((2 * j + crossed) * per, per)
                lane = pl.multiple_of(block * 128, 128)
                copies.append(
                    pltpu.make_async_copy(
                        shards[j * 8 + n],
                        modes.at[pl.ds(row, per), pl.ds(lane, 128)],
                        sems.at[j * 8 + n],
                    )
                )
        for copy in copies:
            copy.start()
        filled = 2 * hops * per
        modes[filled:, :] = jnp.zeros((modes.shape[0] - filled, modes.shape[1]), modes.dtype)
        acc[...] = jnp.zeros_like(acc)
        for copy in copies:
            copy.wait()

    zero_row = 2 * hops * per
    entries = tab_ref.shape[1] - tab_ref.shape[0] * caps

    def source_row(sub, slot, start):
        t = lax.div(slot, caps)
        local = tab_ref[rel_ref[t], entries + sub * caps + (slot - t * caps)]
        row = jnp.where(local < 0, zero_row, rel_ref[t] * per + local * 64)
        return pl.multiple_of(row + start, 16)

    rows = GROUP * WIN
    for e in range(EPS):
        at = step * EPS + e
        sub, blk = own_ref[at], blk_ref[at]
        start = lax.shift_right_logical(off_ref[at], 1) * 16
        lrow = source_row(sub, lax.div(blk, nnz), start)
        rrow = source_row(sub, tab_ref[rel_ref[sub], blk], start)
        lg[e * WIN : (e + 1) * WIN, :] = modes[pl.ds(lrow, WIN), :]
        rg[e * WIN : (e + 1) * WIN, :] = modes[pl.ds(rrow, WIN), 0:256]
    for g in range(STEP):
        for c in range(2):
            yt[c * 256 : (c + 1) * 256, g * rows : (g + 1) * rows] = lax.dot_general(
                rg[g * rows : (g + 1) * rows, :],
                d_ref[g, c],
                (((0,), (1,)), ((), ())),
                preferred_element_type=jnp.float32,
            ).astype(jnp.bfloat16)
    acc[...] += jnp.dot(yt[...], lg[...], preferred_element_type=jnp.float32)

    @pl.when(step == pl.num_programs(0) - 1)
    def _():
        for c in range(2):
            for d, flip in enumerate((0, 2, 1, 3)):
                to = lax.bitwise_xor(me, flip)
                keep_ref[c, to] = acc[c * 256 : c * 256 + 128, d * 128 : (d + 1) * 128].T
                send_ref[c, to] = acc[c * 256 + 128 : c * 256 + 256, d * 128 : (d + 1) * 128].T.astype(
                    jnp.bfloat16
                )


def body(sub_count, col_count, elem_records, elem_owner, elem_block, elem_offset, modes, mode_readers, pattern):
    elems, kw = elem_records.shape
    per_sub, bs, local_cols = modes.shape
    slots, nnz = pattern.shape
    caps = slots // sub_count
    half = sub_count // 2
    ring = line_ring(half)
    place = {z: i for i, z in enumerate(ring)}
    make = functools.partial(permutation, sub_count, col_count)
    to_next = make(lambda s, c: (ring[(place[s // 2] + 1) % half] * 2 + s % 2, c))
    first = make(lambda s, c: (s ^ 1, c) if c % 2 == 0 else (s, c ^ 2))
    second = make(lambda s, c: (s ^ 1, c) if c % 2 == 1 else (s, c ^ 2))
    core = make(lambda s, c: (s, c ^ 1))
    across = make(lambda s, c: (s ^ 1, c))
    over = make(lambda s, c: (s, c ^ 2))
    send = lambda x, pairs: lax.ppermute(x, AXES, pairs)
    me_sub, me_col = lax.axis_index("sub"), lax.axis_index("col")

    readers = mode_readers.reshape(-1)
    order = jnp.arange(readers.shape[0], dtype=jnp.int32)
    same = (readers[:, None] == readers[None, :]) & (order[None, :] < order[:, None])
    rank = jnp.sum(same.astype(jnp.int32), axis=1)
    target = readers * caps + rank
    hit = target[:, None] == jnp.arange(sub_count * caps, dtype=jnp.int32)[None, :]
    table = jnp.sum(jnp.where(hit, order[:, None] // 2 + 1, 0), axis=0) - 1
    packed = jnp.concatenate([pattern.reshape(-1), table])

    places = jnp.stack([elem_owner[:, 0], elem_block, elem_offset])
    places = jnp.concatenate([places, send(places, core)], axis=1)
    records = jnp.concatenate([elem_records, send(elem_records, core)], axis=0)

    rel_place = jnp.asarray([place[z] for z in range(half)], jnp.int32)
    sub_ids = jnp.arange(sub_count, dtype=jnp.int32)
    hops = (rel_place[me_sub // 2] - rel_place[sub_ids // 2]) % half
    rel = hops * 2 + (sub_ids % 2 + me_sub) % 2
    flat = modes.reshape(per_sub * bs, local_cols)
    shards = []
    tables = []
    cur = flat
    for j in range(half):
        if j:
            cur = send(cur, to_next)
            packed = send(packed, to_next)
        a = send(cur, first)
        b0 = send(cur, second)
        b1 = send(a, second)
        shards.append((cur, a, b0, b1))
        tables.append(packed)
    tables = jnp.stack(tables)
    tables = jnp.stack([tables, send(tables, across)], axis=1).reshape(sub_count, -1)

    elem_total = places.shape[1]
    steps = elem_total // EPS
    smem = pl.BlockSpec(memory_space=pltpu.SMEM)
    edof = math.isqrt(kw // 2)
    records = jnp.pad(records.reshape(-1, 2, edof, edof), ((0, 0), (0, 0), (0, 0), (0, 128 - edof)))
    diagonal = pl.pallas_call(
        prep_kernel,
        grid=(steps,),
        in_specs=[smem, pl.BlockSpec((EPS, 2, edof, 128), lambda i: (i, 0, 0, 0))],
        out_specs=pl.BlockSpec((STEP, 2, 256, 256), lambda i: (i, 0, 0, 0)),
        out_shape=jax.ShapeDtypeStruct((steps * STEP, 2, 256, 256), jnp.bfloat16),
        cost_estimate=pl.CostEstimate(flops=10_000_000, bytes_accessed=24_000_000, transcendentals=0),
    )(places[2], records)

    operands = []
    for cur, a, b0, b1 in shards:
        operands += [cur, a, b0, b1] + [send(v, core) for v in (cur, a, b0, b1)]

    modes_rows = sub_count * per_sub * bs + bs + WIN
    hbm = pl.BlockSpec(memory_space=pl.ANY)
    blocked = (2, col_count, 128, 128)
    whole = pl.BlockSpec(blocked, lambda i, *_: (0, 0, 0, 0))
    own, away = pl.pallas_call(
        functools.partial(main_kernel, half, caps, nnz),
        grid_spec=pltpu.PrefetchScalarGridSpec(
            num_scalar_prefetch=6,
            grid=(steps,),
            in_specs=[hbm] * len(operands) + [pl.BlockSpec((STEP, 2, 256, 256), lambda i, *_: (i, 0, 0, 0))],
            out_specs=[whole, whole],
            scratch_shapes=[
                pltpu.VMEM((modes_rows, 4 * local_cols), jnp.bfloat16),
                pltpu.VMEM((EPS * WIN, 4 * local_cols), jnp.bfloat16),
                pltpu.VMEM((EPS * WIN, 256), jnp.bfloat16),
                pltpu.VMEM((512, EPS * WIN), jnp.bfloat16),
                pltpu.VMEM((512, 512), jnp.float32),
                pltpu.SemaphoreType.DMA((len(operands),)),
            ],
        ),
        out_shape=[
            jax.ShapeDtypeStruct(blocked, jnp.float32),
            jax.ShapeDtypeStruct(blocked, jnp.bfloat16),
        ],
        compiler_params=pltpu.CompilerParams(vmem_limit_bytes=60 * 1024 * 1024),
        cost_estimate=pl.CostEstimate(flops=13_000_000_000, bytes_accessed=26_000_000, transcendentals=0),
    )(places[0], places[1], places[2], tables, rel, me_col[None], *operands, diagonal)

    gram = (own + send(away, over).astype(jnp.float32)).astype(jnp.bfloat16)
    gram = gram.reshape(2, sub_count, -1, 128)
    gram = lax.all_to_all(gram, "sub", split_axis=1, concat_axis=1, tiled=True)
    gram = jnp.sum(gram.astype(jnp.float32), axis=1)
    return gram[0], gram[1]


def solution(mesh):
    in_specs = (
        P(AXES, None),
        P(AXES, None),
        P(AXES),
        P(AXES),
        P("sub", None, "col"),
        P("sub", None),
        P("sub", None),
    )
    out_specs = (P("sub", "col"), P("sub", "col"))
    return jax.shard_map(
        functools.partial(body, mesh.shape["sub"], mesh.shape["col"]),
        mesh=mesh,
        in_specs=in_specs,
        out_specs=out_specs,
        check_vma=False,
    )
```
